512 devices in a mesh: side: 2 (over y_hi), group: 64 (over z, y_lo, core), cuts: 4 (over x).
Axes of the slice: x: 4, y: 4 (y_hi: 2, y_lo: 2; y = y_hi * 2 + y_lo), z: 16, core: 2. Of those that a mesh axis runs over, the one named last changes fastest.
Arguments:
- queries: bfloat16 [1024, 4096], P('group', ('side', 'cuts')), may hold values from -8 to 8
- cache_keys: bfloat16 [1024, 8, 64, 512], P('group', ('side', 'cuts')), may hold values from -8 to 8
- cache_values: bfloat16 [1024, 8, 64, 512], P('group', ('side', 'cuts')), may hold values from -6 to 6
- new_keys: bfloat16 [1024, 512], P('group', ('side', 'cuts')), may hold values from -8 to 8
- new_values: bfloat16 [1024, 512], P('group', ('side', 'cuts')), may hold values from -6 to 6
- lengths: int32 [1024], P('group'), may hold values from 1 to 512, as said below
- head_sinks: float32 [64], P(('side', 'cuts')), may hold values from 0 to 6
- attn_proj: bfloat16 [4096, 2880], P(('side', 'cuts'), 'group'), may hold values from -0.625 to 0.625
- residual_in: bfloat16 [1024, 2880], P('group'), may hold values from -8 to 8
- norm_gain: float32 [2880], replicated, may hold values from 0.25 to 1.75
- router: bfloat16 [2880, 32], replicated, may hold values from -0.109375 to 0.109375
- expert_routes: int32 [1024, 4], P('group'), may hold values from 0 to 31, all different within a row; in each aligned block of 16 rows (0 to 15, 16 to 31, ...) at most 4 rows name the same one
- expert_gate: bfloat16 [2880, 92160], P(None, ('side', 'group', 'cuts')), may hold values from -0.109375 to 0.109375
- expert_up: bfloat16 [2880, 92160], P(None, ('side', 'group', 'cuts')), may hold values from -0.109375 to 0.109375
- expert_down: bfloat16 [92160, 2880], P(('side', 'group', 'cuts')), may hold values from -0.109375 to 0.109375
- adapter_in: bfloat16 [2880, 32], replicated, may hold values from -0.109375 to 0.109375
- adapter_gate: bfloat16 [32, 92160], P(None, ('side', 'group', 'cuts')), may hold values from -1 to 1
- adapter_up: bfloat16 [32, 92160], P(None, ('side', 'group', 'cuts')), may hold values from -1 to 1
Outputs:
- hidden_out: bfloat16 [1024, 2880], P('group', 'cuts')
The draws below stay inside these ranges and needn't reach their ends.
Inputs may be any that keep to these rules, and one draw needn't show every extreme that they name: `expert_routes`: the 16 requests of one index of group name any one expert at most 4 times, a bound that some block reaches. `lengths`: some request has all 512 positions valid.
All inputs are finite; a program needn't handle non-finite values.
Results may differ from the reference program's by a relative error of at most 0.02.
Values may be sent and summed in bfloat16 or wider, within the bound.
No kernel may reach another device: no remote copies, remote signals or barrier semaphores. Data moves between devices by JAX's collectives and lax.ppermute only.
A program may use at most 64 MiB of HBM per device.

```python
import math
import jax
import jax.numpy as jnp
import numpy as np
from jax import lax

D = 2880
FF = 2880
EXPERTS = 32
TOPK = 4
HEADS = 64
KV_HEADS = 8
HEAD_DIM = 64
RANK = 32
CACHE = 512
REQ_DEV = 16
CAP = 4
REQUESTS = 1024
N_GROUP = 64


def drawn_floats(key, shape):
    return jnp.clip(jax.random.normal(key, shape, jnp.float32), -6.0, 6.0)


def draw_queries(key, part):
    values = drawn_floats(jax.random.fold_in(key, 11), (REQUESTS, HEADS, HEAD_DIM))
    return values.reshape(REQUESTS, HEADS * HEAD_DIM).astype(jnp.bfloat16)


def draw_cache_keys(key, part):
    values = drawn_floats(jax.random.fold_in(key, 12), (REQUESTS, KV_HEADS, HEAD_DIM, CACHE))
    return values.astype(jnp.bfloat16)


def draw_new_keys(key, part):
    values = drawn_floats(jax.random.fold_in(key, 13), (REQUESTS, KV_HEADS, HEAD_DIM))
    return values.reshape(REQUESTS, KV_HEADS * HEAD_DIM).astype(jnp.bfloat16)


def draw_lengths(key, part):
    drawn = jax.random.randint(jax.random.fold_in(key, 31), (REQUESTS,), 1, CACHE + 1)
    full_at = jax.random.randint(jax.random.fold_in(key, 32), (), 0, REQUESTS)
    return jnp.where(jnp.arange(REQUESTS) == full_at, CACHE, drawn).astype(jnp.int32)


def draw_residual_in(key, part):
    values = 0.5 * jnp.clip(jax.random.normal(jax.random.fold_in(key, 44), (REQUESTS, D), jnp.float32), -6.0, 6.0)
    return values.astype(jnp.bfloat16)


def steps_of(rng, shape, shards, smallest, top_value):
    loudness, own = 1.0, jax.random.fold_in(rng, 6)
    for dim, shards_of in shards:
        steps = jnp.exp(jax.random.uniform(jax.random.fold_in(own, dim), (shards_of,), jnp.float32, smallest / len(shards), top_value / len(shards)))
        loudness = loudness * jnp.repeat(steps, shape[dim] // shards_of).reshape([-1 if axis == dim else 1 for axis in range(len(shape))])
    return loudness


def shared_out(own_key, own, number, rows, number_of, top, limit, lean):
    ranking = jax.random.permutation(own_key, number_of)
    packed, common = shares(number_of, rows * top, limit, lean, True), shares(number_of, rows * top, limit, lean, False)
    places = jnp.arange(number_of)

    def named(sizes, turn):
        used = int((sizes > 0).sum())
        fixed = max(1, used // 4)
        moved = fixed + (places - fixed + turn * (used - fixed)) % max(1, number_of - fixed)
        return jnp.zeros((number_of,), jnp.int32).at[ranking[jnp.where(places < fixed, places, moved)]].set(jnp.asarray(sizes, jnp.int32))

    sizes = jnp.where(number % 4 == 0, named(packed, number // 4), named(common, number - number // 4 - 1))
    mixed = jax.random.permutation(jax.random.fold_in(own, 3), number_of)
    source_of, sink = mixed[0:number_of // 2 * 2:2], mixed[1:number_of // 2 * 2:2]
    margin = jnp.minimum(sizes[source_of] - 1, limit - sizes[sink]) // 2
    margin = jnp.where((source_of == ranking[0]) | (sink == ranking[0]) | (sizes[sink] == 0), 0, jnp.maximum(margin, 0))
    moved = jax.random.randint(jax.random.fold_in(own, 4), (number_of // 2,), 0, 1 << 20) % (margin + 1)
    sizes = sizes.at[source_of].add(-moved).at[sink].add(moved)
    labels = jnp.searchsorted(jnp.cumsum(sizes), jnp.arange(rows * top), side="right").astype(jnp.int32)
    table = labels.reshape(top, rows).T
    table = table[jax.random.permutation(jax.random.fold_in(own, 1), rows)]
    turn = jax.random.randint(jax.random.fold_in(own, 2), (rows, 1), 0, top)
    return jnp.take_along_axis(table, (jnp.arange(top)[None, :] + turn) % top, axis=1)


def shares(amount, total, most, skew, full):
    portions = [(1 << 20) // math.isqrt(grade ** skew) + 1 for grade in range(1, amount + 1)]
    largest = most if full else min(most, max(-(-total // amount), total * portions[0] // sum(portions)))
    least = 1 if total - largest >= amount - 1 else 0
    holding, spare = [largest] + [least] * (amount - 1), total - largest - least * (amount - 1)
    while spare > 0:
        candidates = [i for i in range(1, amount) if holding[i] < largest] or [i for i in range(1, amount) if holding[i] < most]
        mass, remaining = sum([portions[i] for i in candidates]), spare
        for i in candidates:
            extra = min(most - holding[i], max(1, remaining * portions[i] // mass), spare)
            holding[i] = holding[i] + extra
            spare = spare - extra
    return np.array(holding)


def gaussian(stream_key, shape, spread, most, split=(), held_as=jnp.bfloat16):
    values = jax.random.normal(stream_key, shape, jnp.float32) * spread
    if len(split) > 0:
        values = steps_of(stream_key, shape, split, -0.22, 0.18) * values
    return jnp.clip(values, min=-most, max=most).astype(held_as)


def setup_inputs(seed: int = 0) -> dict:
    seeds = jax.random.split(jax.random.key(seed), 19)
    queries = draw_queries(jax.random.fold_in(seeds[18], 71), 0)
    cache_keys = draw_cache_keys(jax.random.fold_in(seeds[18], 71), 0)
    cache_values = gaussian(seeds[2], (REQUESTS, KV_HEADS, HEAD_DIM, CACHE), 1.0, 6.0, ((0, 64), (1, 8)))
    new_keys = draw_new_keys(jax.random.fold_in(seeds[18], 71), 0)
    new_values = gaussian(seeds[4], (REQUESTS, KV_HEADS * HEAD_DIM), 1.0, 6.0, ((0, 64), (1, 8)))
    lengths = draw_lengths(jax.random.fold_in(seeds[18], 71), 0)
    head_sinks = jnp.clip(6.0 * jax.random.uniform(seeds[6], (HEADS,), jnp.float32) ** steps_of(seeds[6], (HEADS,), ((0, 8),), -0.2, 0.2), 0.0, 6.0)
    attn_proj = gaussian(seeds[7], (HEADS * HEAD_DIM, D), 0.1, 0.625, ((0, 8), (1, 64)))
    residual_in = draw_residual_in(jax.random.fold_in(seeds[18], 71), 0)
    norm_gain = jnp.clip(1.0 + 0.15 * jax.random.normal(seeds[9], (D,), jnp.float32), 0.25, 1.75)
    router = gaussian(seeds[10], (D, EXPERTS), D ** -0.5, 0.109375)
    expert_routes_keys = jax.random.split(jax.random.fold_in(seeds[11], 1), REQUESTS // REQ_DEV)
    expert_routes_turns = jax.random.permutation(jax.random.fold_in(seeds[11], 3), REQUESTS // REQ_DEV)
    expert_routes = jax.vmap(lambda own, number: shared_out(jax.random.fold_in(seeds[11], 2), own, number, REQ_DEV, EXPERTS, TOPK, CAP, 2))(expert_routes_keys, expert_routes_turns).reshape((REQUESTS, TOPK))
    expert_gate = gaussian(seeds[12], (D, EXPERTS * FF), D ** -0.5, 0.109375, ((1, 512),))
    expert_up = gaussian(seeds[13], (D, EXPERTS * FF), D ** -0.5, 0.109375, ((1, 512),))
    expert_down = gaussian(seeds[14], (EXPERTS * FF, D), FF ** -0.5, 0.109375, ((0, 512),))
    adapter_in = gaussian(seeds[15], (D, RANK), D ** -0.5, 0.109375)
    adapter_gate = gaussian(seeds[16], (RANK, EXPERTS * FF), RANK ** -0.5, 1.0, ((1, 512),))
    adapter_up = gaussian(seeds[17], (RANK, EXPERTS * FF), RANK ** -0.5, 1.0, ((1, 512),))
    return dict(queries=queries, cache_keys=cache_keys, cache_values=cache_values, new_keys=new_keys, new_values=new_values, lengths=lengths, head_sinks=head_sinks, attn_proj=attn_proj, residual_in=residual_in, norm_gain=norm_gain, router=router, expert_routes=expert_routes, expert_gate=expert_gate, expert_up=expert_up, expert_down=expert_down, adapter_in=adapter_in, adapter_gate=adapter_gate, adapter_up=adapter_up)


def attention_rows(queries, cache_keys, cache_values, new_keys, new_values, lengths, head_sinks):
    req_count = queries.shape[0]
    kv_count = cache_keys.shape[1]
    head_dim = cache_keys.shape[2]
    cache_len = cache_keys.shape[3]
    head_count = head_sinks.shape[0]
    group_size = head_count // kv_count
    query_rows = queries.reshape(req_count, kv_count, group_size, head_dim).astype(jnp.float32)
    fresh_key = new_keys.reshape(req_count, kv_count, head_dim).astype(jnp.float32)
    fresh_value = new_values.reshape(req_count, kv_count, head_dim).astype(jnp.float32)
    scaling = 1.0 / math.sqrt(head_dim)
    scores = jnp.einsum('rkgd,rkdl->rkgl', query_rows, cache_keys.astype(jnp.float32)) * scaling
    own_score = jnp.einsum('rkgd,rkd->rkg', query_rows, fresh_key) * scaling
    validity = lax.broadcasted_iota(jnp.int32, (req_count, 1, 1, cache_len), 3) < lengths[:, None, None, None]
    scores = jnp.where(validity, scores, -1e+30)
    sink_logit = head_sinks.reshape(1, kv_count, group_size)
    highest = jnp.maximum(jnp.maximum(lax.optimization_barrier(jnp.max(scores, axis=3)), own_score), sink_logit)
    exp_terms = jnp.where(validity, jnp.exp(scores - highest[..., None]), 0.0)
    own_term = jnp.exp(own_score - highest)
    denominator = lax.optimization_barrier(jnp.sum(exp_terms, axis=3)) + own_term + jnp.exp(sink_logit - highest)
    attn_probs = (exp_terms / denominator[..., None]).astype(jnp.bfloat16)
    own_prob = (own_term / denominator).astype(jnp.bfloat16)
    attn_mix = jnp.einsum('rkgl,rkdl->rkgd', attn_probs.astype(jnp.float32), cache_values.astype(jnp.float32))
    attn_mix = attn_mix + own_prob.astype(jnp.float32)[..., None] * fresh_value[:, :, None, :]
    return attn_mix.astype(jnp.bfloat16).reshape(req_count, head_count * head_dim)

def reference(queries, cache_keys, cache_values, new_keys, new_values, lengths, head_sinks, attn_proj, residual_in, norm_gain, router, expert_routes, expert_gate, expert_up, expert_down, adapter_in, adapter_gate, adapter_up):
    attn_out = attention_rows(queries, cache_keys, cache_values, new_keys, new_values, lengths, head_sinks)
    projected = jnp.dot(attn_out, attn_proj, preferred_element_type=jnp.float32)
    middle = residual_in.astype(jnp.float32) + projected
    inverse = lax.rsqrt(lax.optimization_barrier(jnp.mean(middle * middle, axis=1, keepdims=True)) + 1e-05)
    normed = (middle * inverse * norm_gain).astype(jnp.bfloat16)
    logits = jnp.dot(normed, router, preferred_element_type=jnp.float32)
    picked = jnp.take_along_axis(logits, expert_routes, axis=1)
    raw_gate = jax.nn.sigmoid(picked)
    gate_weights = raw_gate / lax.optimization_barrier(jnp.sum(raw_gate, axis=1, keepdims=True))
    low_code = jnp.dot(normed, adapter_in, preferred_element_type=jnp.float32).astype(jnp.bfloat16)
    capacity = N_GROUP * CAP

    def one_expert(moe_sum, expert):
        matched = expert_routes == expert
        weight_rows = lax.optimization_barrier(jnp.sum(jnp.where(matched, gate_weights, 0.0), axis=1))
        member = jnp.any(matched, axis=1)
        picks = jnp.nonzero(member, size=capacity, fill_value=0)[0].astype(jnp.int32)
        live = jnp.arange(capacity) < jnp.sum(member.astype(jnp.int32))
        row_weight = jnp.where(live, weight_rows[picks], 0.0)
        rows_in = normed[picks]
        rows_code = low_code[picks]
        first_col = (expert * FF).astype(jnp.int32)
        pre_gate = jnp.dot(rows_in, lax.dynamic_slice_in_dim(expert_gate, first_col, FF, 1), preferred_element_type=jnp.float32)
        pre_gate = pre_gate + jnp.dot(rows_code, lax.dynamic_slice_in_dim(adapter_gate, first_col, FF, 1), preferred_element_type=jnp.float32)
        pre_up = jnp.dot(rows_in, lax.dynamic_slice_in_dim(expert_up, first_col, FF, 1), preferred_element_type=jnp.float32)
        pre_up = pre_up + jnp.dot(rows_code, lax.dynamic_slice_in_dim(adapter_up, first_col, FF, 1), preferred_element_type=jnp.float32)
        activated = ((pre_up + 1.0) * pre_gate * jax.nn.sigmoid(1.702 * pre_gate)).astype(jnp.bfloat16)
        out_rows = jnp.dot(activated, lax.dynamic_slice_in_dim(expert_down, first_col, FF, 0), preferred_element_type=jnp.float32)
        moe_sum = moe_sum.at[picks].add(out_rows * row_weight[:, None])
        return (moe_sum, None)
    moe, unused = lax.scan(one_expert, jnp.zeros((REQUESTS, D), jnp.float32), jnp.arange(EXPERTS, dtype=jnp.int32))
    return (middle + moe).astype(jnp.bfloat16)
```

```python
import math

import jax
import jax.numpy as jnp
from jax import lax
from jax.sharding import Mesh, PartitionSpec as P

CAP = 4
EPSILON = 1e-05
F32 = jnp.float32
BF16 = jnp.bfloat16


def attention_rows(queries, cache_keys, cache_values, new_keys, new_values, lengths, head_sinks):
    req_count = queries.shape[0]
    kv_count = cache_keys.shape[1]
    head_dim = cache_keys.shape[2]
    cache_len = cache_keys.shape[3]
    head_count = head_sinks.shape[0]
    group_size = head_count // kv_count
    query_rows = queries.reshape(req_count, kv_count, group_size, head_dim)
    fresh_key = new_keys.reshape(req_count, kv_count, head_dim)
    fresh_value = new_values.reshape(req_count, kv_count, head_dim)
    scaling = 1.0 / math.sqrt(head_dim)
    scores = (
        jnp.einsum("rkgd,rkdl->rkgl", query_rows, cache_keys, preferred_element_type=F32) * scaling
    )
    own_score = (
        jnp.einsum("rkgd,rkd->rkg", query_rows, fresh_key, preferred_element_type=F32) * scaling
    )
    validity = (
        lax.broadcasted_iota(jnp.int32, (req_count, 1, 1, cache_len), 3)
        < lengths[:, None, None, None]
    )
    scores = jnp.where(validity, scores, -1e30)
    sink_logit = head_sinks.reshape(1, kv_count, group_size)
    highest = jnp.maximum(jnp.maximum(jnp.max(scores, axis=3), own_score), sink_logit)
    exp_terms = jnp.where(validity, jnp.exp(scores - highest[..., None]), 0.0)
    own_term = jnp.exp(own_score - highest)
    denominator = jnp.sum(exp_terms, axis=3) + own_term + jnp.exp(sink_logit - highest)
    attn_probs = (exp_terms / denominator[..., None]).astype(BF16)
    own_prob = (own_term / denominator).astype(BF16)
    attn_mix = jnp.einsum("rkgl,rkdl->rkgd", attn_probs, cache_values, preferred_element_type=F32)
    attn_mix = attn_mix + own_prob.astype(F32)[..., None] * fresh_value.astype(F32)[:, :, None, :]
    return attn_mix.astype(BF16).reshape(req_count, head_count * head_dim)


def exchange(array, axes):
    return lax.all_to_all(array, axes, split_axis=0, concat_axis=0, tiled=True)


def slot_hot(routes, experts):
    rows = routes.shape[1]
    member = jnp.any(routes[None] == experts[:, None, None, None], axis=3)
    earlier = (
        lax.broadcasted_iota(jnp.int32, (rows, rows), 0)
        < lax.broadcasted_iota(jnp.int32, (rows, rows), 1)
    ).astype(BF16)
    before = jnp.einsum(
        "ebr,rq->ebq", member.astype(BF16), earlier, preferred_element_type=F32
    ).astype(jnp.int32)
    slots = lax.broadcasted_iota(jnp.int32, (1, 1, CAP, 1), 2)
    return (member[:, :, None, :] & (before[:, :, None, :] == slots)).astype(BF16)


def shards(
    queries,
    cache_keys,
    cache_values,
    new_keys,
    new_values,
    lengths,
    head_sinks,
    attn_proj,
    residual_in,
    norm_gain,
    router,
    expert_routes,
    expert_gate,
    expert_up,
    expert_down,
    adapter_in,
    adapter_gate,
    adapter_up,
):
    planes = lax.axis_size("z")
    n_cuts = lax.axis_size("cuts")
    n_side = lax.axis_size("side")
    n_ylo = lax.axis_size("ylo")
    side = lax.axis_index("side")
    plane = lax.axis_index("z")
    ylo = lax.axis_index("ylo")
    cut = lax.axis_index("cuts")
    rows, width = residual_in.shape
    topk = expert_routes.shape[1]
    heads_in, piece = attn_proj.shape
    strip = width // planes
    quarter = width // n_cuts
    swap = [(0, 1), (1, 0)]

    plane_proj = exchange(
        jnp.broadcast_to(attn_proj.T[None], (4, piece, heads_in)), ("ylo", "core")
    ).reshape(strip, heads_in)
    gate_t = jnp.concatenate([expert_gate.T, lax.ppermute(expert_gate.T, "core", swap)], 0)
    up_t = jnp.concatenate([expert_up.T, lax.ppermute(expert_up.T, "core", swap)], 0)
    down = jnp.concatenate([expert_down, lax.ppermute(expert_down, "core", swap)], 0)
    adapt_gate = jnp.concatenate([adapter_gate, lax.ppermute(adapter_gate, "core", swap)], 1)
    adapt_up = jnp.concatenate([adapter_up, lax.ppermute(adapter_up, "core", swap)], 1)

    attn_out = attention_rows(
        queries, cache_keys, cache_values, new_keys, new_values, lengths, head_sinks
    )

    residual = residual_in.reshape(rows, planes, n_cuts, piece)
    residual = lax.dynamic_index_in_dim(residual, cut, 2, keepdims=False).transpose(1, 0, 2)
    payload = jnp.concatenate(
        [
            jnp.broadcast_to(attn_out[None], (planes, rows, heads_in)),
            residual,
            jnp.broadcast_to(expert_routes.astype(BF16)[None], (planes, rows, topk)),
            jnp.zeros((planes, rows, 128 - piece - topk), BF16),
        ],
        axis=2,
    )
    held = exchange(payload, "z").reshape(planes * rows, heads_in + 128)
    line = lax.broadcasted_iota(jnp.int32, (strip, 128), 1)
    column = lax.broadcasted_iota(jnp.int32, (strip, 128), 0)
    residual_part = jnp.where((column == cut * piece + line) & (line < piece), 1.0 / n_side, 0.0)
    weights = jnp.concatenate([plane_proj, residual_part.astype(BF16)], 1)
    partial = lax.dot_general(held, weights, (((1,), (1,)), ((), ())), preferred_element_type=F32)
    partial = partial.astype(BF16).reshape(1, n_cuts, rows * planes // n_cuts, strip)
    partial = jnp.broadcast_to(partial, (n_side,) + partial.shape[1:])
    partial = exchange(partial.reshape((n_side * n_cuts,) + partial.shape[2:]), ("side", "cuts"))
    middle = jnp.sum(partial.astype(F32), axis=0).astype(BF16)

    blocks = planes // n_cuts
    experts = side * planes + jnp.arange(planes)
    routes = held[:, heads_in + piece : heads_in + piece + topk].reshape(n_cuts, blocks, rows, topk)
    routes = lax.dynamic_index_in_dim(routes, cut, 0, keepdims=False)
    hot = slot_hot(routes.astype(jnp.int32), experts)
    source = jnp.concatenate([middle.reshape(blocks, rows, strip), routes], 2)
    outgoing = jnp.einsum("zktr,krd->zktd", hot, source, preferred_element_type=F32).astype(BF16)
    outgoing = outgoing.reshape(planes, blocks * CAP, strip + topk)
    arrived = exchange(outgoing, "z")
    row_part = arrived[:, :, :strip].transpose(1, 0, 2).reshape(blocks * CAP, width)
    row_part = jnp.concatenate([row_part, arrived[0, :, strip:]], 1)
    peers = n_ylo * n_cuts
    row_block = exchange(jnp.broadcast_to(row_part[None], (peers,) + row_part.shape), ("ylo", "cuts"))
    row_block = row_block.reshape(-1, width + topk)

    middle_rows = row_block[:, :width].astype(F32)
    row_routes = row_block[:, width:].astype(jnp.int32)
    inverse = lax.rsqrt(jnp.mean(middle_rows * middle_rows, axis=1, keepdims=True) + EPSILON)
    normed = (middle_rows * inverse * norm_gain).astype(BF16)
    raw = jax.nn.sigmoid(jnp.dot(normed, router, preferred_element_type=F32))
    expert = side * planes + plane
    names = lax.broadcasted_iota(jnp.int32, (1, router.shape[1]), 1)
    named = jnp.any(row_routes[:, :, None] == names[:, None, :], axis=1)
    row_weight = jnp.sum(jnp.where(names == expert, raw, 0.0), axis=1) / jnp.sum(
        jnp.where(named, raw, 0.0), axis=1
    )
    first = (row_routes[:, 0] == expert).astype(F32)
    low_code = jnp.dot(normed, adapter_in, preferred_element_type=F32).astype(BF16)
    nt = (((1,), (1,)), ((), ()))
    pre_gate = lax.dot_general(normed, gate_t, nt, preferred_element_type=F32)
    pre_gate = pre_gate + jnp.dot(low_code, adapt_gate, preferred_element_type=F32)
    pre_up = lax.dot_general(normed, up_t, nt, preferred_element_type=F32)
    pre_up = pre_up + jnp.dot(low_code, adapt_up, preferred_element_type=F32)
    activated = ((pre_up + 1.0) * pre_gate * jax.nn.sigmoid(1.702 * pre_gate)).astype(BF16)
    value = jnp.dot(activated, down, preferred_element_type=F32).astype(BF16)

    own_rows = value.shape[0] // n_ylo
    value = value.reshape(n_ylo, own_rows, n_cuts, quarter).transpose(0, 2, 1, 3)
    value = exchange(value.reshape(peers, own_rows, quarter), ("ylo", "cuts"))
    total = jnp.sum(value.astype(F32), axis=0)
    own_weight = lax.dynamic_slice_in_dim(row_weight, ylo * own_rows, own_rows)
    own_first = lax.dynamic_slice_in_dim(first, ylo * own_rows, own_rows)
    own_middle = lax.dynamic_slice(
        row_block, (ylo * own_rows, cut * quarter), (own_rows, quarter)
    ).astype(F32)
    total = (total * own_weight[:, None] + own_middle * own_first[:, None]).astype(BF16)
    returned = exchange(total.reshape(planes, CAP, quarter), "z")
    own_hot = slot_hot(expert_routes[None], experts)[:, 0]
    out = jnp.einsum("ztr,ztd->rd", own_hot, returned, preferred_element_type=F32).astype(BF16)
    other = lax.ppermute(out, "side", swap)
    return (out.astype(F32) + other.astype(F32)).astype(BF16)


def solution(mesh):
    fine = Mesh(mesh.devices.reshape(2, 16, 2, 2, 4), ("side", "z", "ylo", "core", "cuts"))
    group = ("z", "ylo", "core")
    heads = ("side", "cuts")
    hidden = ("side", "z", "ylo", "core", "cuts")
    placed = (
        P(group, heads),
        P(group, heads, None, None),
        P(group, heads, None, None),
        P(group, heads),
        P(group, heads),
        P(group),
        P(heads),
        P(heads, group),
        P(group, None),
        P(),
        P(),
        P(group, None),
        P(None, hidden),
        P(None, hidden),
        P(hidden, None),
        P(),
        P(None, hidden),
        P(None, hidden),
    )
    return jax.shard_map(
        shards, mesh=fine, in_specs=placed, out_specs=P(group, "cuts"), check_vma=False
    )
```

```python
import functools
import math

import jax
import jax.numpy as jnp
from jax import lax
from jax.experimental import pallas as pl
from jax.experimental.pallas import tpu as pltpu
from jax.sharding import Mesh, PartitionSpec as P

CAP = 4
EPSILON = 1e-05
F32 = jnp.float32
BF16 = jnp.bfloat16


def attention_rows(queries, cache_keys, cache_values, new_keys, new_values, lengths, head_sinks):
    req_count = queries.shape[0]
    kv_count = cache_keys.shape[1]
    head_dim = cache_keys.shape[2]
    cache_len = cache_keys.shape[3]
    head_count = head_sinks.shape[0]
    group_size = head_count // kv_count
    query_rows = queries.reshape(req_count, kv_count, group_size, head_dim)
    fresh_key = new_keys.reshape(req_count, kv_count, head_dim)
    fresh_value = new_values.reshape(req_count, kv_count, head_dim)
    scaling = 1.0 / math.sqrt(head_dim)
    scores = (
        jnp.einsum("rkgd,rkdl->rkgl", query_rows, cache_keys, preferred_element_type=F32) * scaling
    )
    own_score = (
        jnp.einsum("rkgd,rkd->rkg", query_rows, fresh_key, preferred_element_type=F32) * scaling
    )
    validity = (
        lax.broadcasted_iota(jnp.int32, (req_count, 1, 1, cache_len), 3)
        < lengths[:, None, None, None]
    )
    scores = jnp.where(validity, scores, -1e30)
    sink_logit = head_sinks.reshape(1, kv_count, group_size)
    highest = jnp.maximum(jnp.maximum(jnp.max(scores, axis=3), own_score), sink_logit)
    exp_terms = jnp.where(validity, jnp.exp(scores - highest[..., None]), 0.0)
    own_term = jnp.exp(own_score - highest)
    denominator = jnp.sum(exp_terms, axis=3) + own_term + jnp.exp(sink_logit - highest)
    attn_probs = (exp_terms / denominator[..., None]).astype(BF16)
    own_prob = (own_term / denominator).astype(BF16)
    attn_mix = jnp.einsum("rkgl,rkdl->rkgd", attn_probs, cache_values, preferred_element_type=F32)
    attn_mix = attn_mix + own_prob.astype(F32)[..., None] * fresh_value.astype(F32)[:, :, None, :]
    return attn_mix.astype(BF16).reshape(req_count, head_count * head_dim)


def exchange(array, axes):
    return lax.all_to_all(array, axes, split_axis=0, concat_axis=0, tiled=True)


def slot_hot(routes, experts):
    rows = routes.shape[1]
    member = jnp.any(routes[None] == experts[:, None, None, None], axis=3)
    earlier = (
        lax.broadcasted_iota(jnp.int32, (rows, rows), 0)
        < lax.broadcasted_iota(jnp.int32, (rows, rows), 1)
    ).astype(BF16)
    before = jnp.einsum(
        "ebr,rq->ebq", member.astype(BF16), earlier, preferred_element_type=F32
    ).astype(jnp.int32)
    slots = lax.broadcasted_iota(jnp.int32, (1, 1, CAP, 1), 2)
    return (member[:, :, None, :] & (before[:, :, None, :] == slots)).astype(BF16)


def expert_kernel(n_ylo, n_cuts, topk, *refs):
    (expert_ref, rows_ref, gain_ref, router_ref, low_ref, *rest) = refs
    adapters, weights = rest[:2], rest[2:8]
    out_ref, held, sems = rest[8:]
    copies = [
        pltpu.make_async_copy(weights[i], held.at[i], sems.at[i]) for i in range(len(weights))
    ]
    for copy in copies:
        copy.start()
    width = gain_ref.shape[1]
    quarter = width // n_cuts
    nt = (((1,), (1,)), ((), ()))
    middle = rows_ref[:, :width].astype(F32)
    inverse = lax.rsqrt(jnp.mean(middle * middle, axis=1, keepdims=True) + EPSILON)
    normed = (middle * inverse * gain_ref[...]).astype(BF16)
    raw = jax.nn.sigmoid(lax.dot_general(normed, router_ref[...], nt, preferred_element_type=F32))
    names = lax.broadcasted_iota(jnp.int32, raw.shape, 1)
    named = names < 0
    for entry in range(topk):
        route = rows_ref[:, width + entry : width + entry + 1].astype(F32).astype(jnp.int32)
        named = named | (names == route)
    own = jnp.sum(jnp.where(names == expert_ref[0], raw, 0.0), axis=1, keepdims=True)
    row_weight = own / jnp.sum(jnp.where(named, raw, 0.0), axis=1, keepdims=True)
    low_code = lax.dot_general(normed, low_ref[...], nt, preferred_element_type=F32).astype(BF16)
    rank = low_ref.shape[0]
    total = None
    for half in range(2):
        copies[3 * half].wait()
        pre_gate = lax.dot_general(normed, held[3 * half], nt, preferred_element_type=F32)
        pre_gate = pre_gate + jnp.dot(
            low_code, adapters[half][:rank], preferred_element_type=F32
        )
        copies[3 * half + 1].wait()
        pre_up = lax.dot_general(normed, held[3 * half + 1], nt, preferred_element_type=F32)
        pre_up = pre_up + jnp.dot(low_code, adapters[half][rank:], preferred_element_type=F32)
        activated = (pre_up + 1.0) * pre_gate * jax.nn.sigmoid(1.702 * pre_gate)
        copies[3 * half + 2].wait()
        part = jnp.dot(activated.astype(BF16), held[3 * half + 2], preferred_element_type=F32)
        total = part if total is None else total + part
    total = total * row_weight
    own_rows = total.shape[0] // n_ylo
    for peer in range(n_ylo * n_cuts):
        row, column = peer // n_cuts * own_rows, peer % n_cuts * quarter
        out_ref[peer] = total[row : row + own_rows, column : column + quarter].astype(BF16)


def expert_rows(row_block, own, other, norm_gain, router, adapter_in, expert, counts):
    n_ylo, n_cuts, topk = counts
    width = norm_gain.shape[0]
    rows = row_block.shape[0]
    whole = pl.BlockSpec(memory_space=pltpu.VMEM)
    weights = own[:3] + other[:3]
    return pl.pallas_call(
        functools.partial(expert_kernel, n_ylo, n_cuts, topk),
        out_shape=jax.ShapeDtypeStruct((n_ylo * n_cuts, rows // n_ylo, width // n_cuts), BF16),
        in_specs=[pl.BlockSpec(memory_space=pltpu.SMEM)]
        + [whole] * 6
        + [pl.BlockSpec(memory_space=pl.ANY)] * len(weights),
        out_specs=whole,
        scratch_shapes=[
            pltpu.VMEM((len(weights),) + weights[0].shape, BF16),
            pltpu.SemaphoreType.DMA((len(weights),)),
        ],
        name="expert_rows",
    )(
        expert.reshape(1).astype(jnp.int32),
        row_block,
        norm_gain[None],
        router.T,
        adapter_in.T,
        own[3],
        other[3],
        *weights,
    )


def shards(
    queries,
    cache_keys,
    cache_values,
    new_keys,
    new_values,
    lengths,
    head_sinks,
    attn_proj,
    residual_in,
    norm_gain,
    router,
    expert_routes,
    expert_gate,
    expert_up,
    expert_down,
    adapter_in,
    adapter_gate,
    adapter_up,
):
    planes = lax.axis_size("z")
    n_cuts = lax.axis_size("cuts")
    n_side = lax.axis_size("side")
    n_ylo = lax.axis_size("ylo")
    side = lax.axis_index("side")
    plane = lax.axis_index("z")
    ylo = lax.axis_index("ylo")
    cut = lax.axis_index("cuts")
    rows, width = residual_in.shape
    topk = expert_routes.shape[1]
    heads_in, piece = attn_proj.shape
    strip = width // planes
    quarter = width // n_cuts
    swap = [(0, 1), (1, 0)]

    pieces = [attn_proj.T]
    for axes in ("core", "ylo", ("ylo", "core")):
        flip = swap if isinstance(axes, str) else [(i, 3 - i) for i in range(4)]
        pieces.append(lax.ppermute(attn_proj.T, axes, flip))
    core = lax.axis_index("core")
    pieces = [jnp.where(core == 0, pieces[i], pieces[i ^ 1]) for i in range(4)]
    pieces = [jnp.where(ylo == 0, pieces[i], pieces[i ^ 2]) for i in range(4)]
    plane_proj = jnp.concatenate(pieces, 0)
    adapters = jnp.concatenate([adapter_gate, adapter_up], 0)
    hidden_own = (expert_gate.T, expert_up.T, expert_down, adapters)
    hidden_other = tuple(lax.ppermute(part, "core", swap) for part in hidden_own)

    attn_out = attention_rows(
        queries, cache_keys, cache_values, new_keys, new_values, lengths, head_sinks
    )

    residual = residual_in.reshape(rows, planes, n_cuts, piece)
    residual = lax.dynamic_index_in_dim(residual, cut, 2, keepdims=False).transpose(1, 0, 2)
    payload = jnp.concatenate(
        [
            jnp.broadcast_to(attn_out[None], (planes, rows, heads_in)),
            residual,
            jnp.broadcast_to(expert_routes.astype(BF16)[None], (planes, rows, topk)),
            jnp.zeros((planes, rows, 128 - piece - topk), BF16),
        ],
        axis=2,
    )
    held = exchange(payload, "z")
    held = held.reshape(planes * rows, heads_in + 128)
    line = lax.broadcasted_iota(jnp.int32, (strip, 128), 1)
    column = lax.broadcasted_iota(jnp.int32, (strip, 128), 0)
    residual_part = jnp.where((column == cut * piece + line) & (line < piece), 1.0 / n_side, 0.0)
    weights = jnp.concatenate([plane_proj, residual_part.astype(BF16)], 1)
    partial = lax.dot_general(held, weights, (((1,), (1,)), ((), ())), preferred_element_type=F32)
    partial = partial.astype(BF16).reshape(1, n_cuts, rows * planes // n_cuts, strip)
    partial = jnp.broadcast_to(partial, (n_side,) + partial.shape[1:])
    partial = exchange(partial.reshape((n_side * n_cuts,) + partial.shape[2:]), ("side", "cuts"))
    middle = jnp.sum(partial.astype(F32), axis=0).astype(BF16)

    blocks = planes // n_cuts
    experts = side * planes + jnp.arange(planes)
    routes = held[:, heads_in + piece : heads_in + piece + topk].reshape(n_cuts, blocks, rows, topk)
    routes = lax.dynamic_index_in_dim(routes, cut, 0, keepdims=False)
    hot = slot_hot(routes.astype(jnp.int32), experts)
    source = jnp.concatenate([middle.reshape(blocks, rows, strip), routes], 2)
    outgoing = jnp.einsum("zktr,krd->zktd", hot, source, preferred_element_type=F32).astype(BF16)
    outgoing = outgoing.reshape(planes, blocks * CAP, strip + topk)
    arrived = exchange(outgoing, "z")
    row_part = arrived[:, :, :strip].transpose(1, 0, 2).reshape(blocks * CAP, width)
    lanes = -(-(width + topk) // 128) * 128
    spare = jnp.zeros((blocks * CAP, lanes - width - topk), BF16)
    row_part = jnp.concatenate([row_part, arrived[0, :, strip:], spare], 1)
    peers = n_ylo * n_cuts
    row_block = exchange(jnp.broadcast_to(row_part[None], (peers,) + row_part.shape), ("ylo", "cuts"))
    row_block = row_block.reshape(-1, lanes)

    expert = side * planes + plane
    value = expert_rows(
        row_block,
        hidden_own,
        hidden_other,
        norm_gain,
        router,
        adapter_in,
        expert,
        (n_ylo, n_cuts, topk),
    )

    own_rows = row_block.shape[0] // n_ylo
    value = exchange(value, ("ylo", "cuts"))
    total = jnp.sum(value.astype(F32), axis=0)
    mine = lax.dynamic_slice_in_dim(row_block, ylo * own_rows, own_rows)
    first = (mine[:, width].astype(jnp.int32) == expert).astype(F32)
    own_middle = lax.dynamic_slice_in_dim(mine, cut * quarter, quarter, 1).astype(F32)
    total = (total + own_middle * first[:, None]).astype(BF16)
    total = jnp.broadcast_to(total.reshape(1, planes, CAP, quarter), (n_side, planes, CAP, quarter))
    returned = exchange(total.reshape(n_side * planes, CAP, quarter), ("side", "z"))
    own_hot = slot_hot(expert_routes[None], jnp.arange(n_side * planes))[:, 0]
    out = jnp.einsum("etr,etd->rd", own_hot, returned, preferred_element_type=F32)
    return out.astype(BF16)


def solution(mesh):
    fine = Mesh(mesh.devices.reshape(2, 16, 2, 2, 4), ("side", "z", "ylo", "core", "cuts"))
    group = ("z", "ylo", "core")
    heads = ("side", "cuts")
    hidden = ("side", "z", "ylo", "core", "cuts")
    placed = (
        P(group, heads),
        P(group, heads, None, None),
        P(group, heads, None, None),
        P(group, heads),
        P(group, heads),
        P(group),
        P(heads),
        P(heads, group),
        P(group, None),
        P(),
        P(),
        P(group, None),
        P(None, hidden),
        P(None, hidden),
        P(hidden, None),
        P(),
        P(None, hidden),
        P(None, hidden),
    )

    return jax.shard_map(
        shards, mesh=fine, in_specs=placed, out_specs=P(group, "cuts"), check_vma=False
    )
```

```python
import functools
import math

import jax
import jax.numpy as jnp
from jax import lax
from jax.experimental import pallas as pl
from jax.experimental.pallas import tpu as pltpu
from jax.sharding import Mesh, PartitionSpec as P

CAP = 4
EPSILON = 1e-05
F32 = jnp.float32
BF16 = jnp.bfloat16


def attention_rows(queries, cache_keys, cache_values, new_keys, new_values, lengths, head_sinks):
    req_count = queries.shape[0]
    kv_count = cache_keys.shape[1]
    head_dim = cache_keys.shape[2]
    cache_len = cache_keys.shape[3]
    head_count = head_sinks.shape[0]
    group_size = head_count // kv_count
    query_rows = queries.reshape(req_count, kv_count, group_size, head_dim)
    fresh_key = new_keys.reshape(req_count, kv_count, head_dim)
    fresh_value = new_values.reshape(req_count, kv_count, head_dim)
    scaling = 1.0 / math.sqrt(head_dim)
    scores = (
        jnp.einsum("rkgd,rkdl->rkgl", query_rows, cache_keys, preferred_element_type=F32) * scaling
    )
    own_score = (
        jnp.einsum("rkgd,rkd->rkg", query_rows, fresh_key, preferred_element_type=F32) * scaling
    )
    validity = (
        lax.broadcasted_iota(jnp.int32, (req_count, 1, 1, cache_len), 3)
        < lengths[:, None, None, None]
    )
    scores = jnp.where(validity, scores, -1e30)
    sink_logit = head_sinks.reshape(1, kv_count, group_size)
    highest = jnp.maximum(jnp.maximum(jnp.max(scores, axis=3), own_score), sink_logit)
    exp_terms = jnp.where(validity, jnp.exp(scores - highest[..., None]), 0.0)
    own_term = jnp.exp(own_score - highest)
    denominator = jnp.sum(exp_terms, axis=3) + own_term + jnp.exp(sink_logit - highest)
    attn_probs = (exp_terms / denominator[..., None]).astype(BF16)
    own_prob = (own_term / denominator).astype(BF16)
    attn_mix = jnp.einsum("rkgl,rkdl->rkgd", attn_probs, cache_values, preferred_element_type=F32)
    attn_mix = attn_mix + own_prob.astype(F32)[..., None] * fresh_value.astype(F32)[:, :, None, :]
    return attn_mix.astype(BF16).reshape(req_count, head_count * head_dim)


def exchange(array, axes):
    return lax.all_to_all(array, axes, split_axis=0, concat_axis=0, tiled=True)


def slot_hot(routes, experts):
    rows = routes.shape[1]
    member = jnp.any(routes[None] == experts[:, None, None, None], axis=3)
    earlier = (
        lax.broadcasted_iota(jnp.int32, (rows, rows), 0)
        < lax.broadcasted_iota(jnp.int32, (rows, rows), 1)
    ).astype(BF16)
    before = jnp.einsum(
        "ebr,rq->ebq", member.astype(BF16), earlier, preferred_element_type=F32
    ).astype(jnp.int32)
    slots = lax.broadcasted_iota(jnp.int32, (1, 1, CAP, 1), 2)
    return (member[:, :, None, :] & (before[:, :, None, :] == slots)).astype(BF16)


def expert_kernel(n_ylo, n_cuts, topk, *refs):
    (expert_ref, rows_ref, gain_ref, router_ref, low_ref, *rest) = refs
    adapters, weights = rest[:2], rest[2:8]
    out_ref, held, sems = rest[8:]
    copies = [
        pltpu.make_async_copy(weights[i], held.at[i], sems.at[i]) for i in range(len(weights))
    ]
    for copy in copies:
        copy.start()
    width = gain_ref.shape[1]
    quarter = width // n_cuts
    nt = (((1,), (1,)), ((), ()))
    middle = rows_ref[:, :width].astype(F32)
    inverse = lax.rsqrt(jnp.mean(middle * middle, axis=1, keepdims=True) + EPSILON)
    normed = (middle * inverse * gain_ref[...]).astype(BF16)
    raw = jax.nn.sigmoid(lax.dot_general(normed, router_ref[...], nt, preferred_element_type=F32))
    names = lax.broadcasted_iota(jnp.int32, raw.shape, 1)
    named = names < 0
    for entry in range(topk):
        route = rows_ref[:, width + entry : width + entry + 1].astype(F32).astype(jnp.int32)
        named = named | (names == route)
    own = jnp.sum(jnp.where(names == expert_ref[0], raw, 0.0), axis=1, keepdims=True)
    row_weight = own / jnp.sum(jnp.where(named, raw, 0.0), axis=1, keepdims=True)
    low_code = lax.dot_general(normed, low_ref[...], nt, preferred_element_type=F32).astype(BF16)
    rank = low_ref.shape[0]
    total = None
    for half in range(2):
        copies[3 * half].wait()
        pre_gate = lax.dot_general(normed, held[3 * half], nt, preferred_element_type=F32)
        pre_gate = pre_gate + jnp.dot(
            low_code, adapters[half][:rank], preferred_element_type=F32
        )
        copies[3 * half + 1].wait()
        pre_up = lax.dot_general(normed, held[3 * half + 1], nt, preferred_element_type=F32)
        pre_up = pre_up + jnp.dot(low_code, adapters[half][rank:], preferred_element_type=F32)
        activated = (pre_up + 1.0) * pre_gate * jax.nn.sigmoid(1.702 * pre_gate)
        copies[3 * half + 2].wait()
        part = jnp.dot(activated.astype(BF16), held[3 * half + 2], preferred_element_type=F32)
        total = part if total is None else total + part
    total = total * row_weight
    own_rows = total.shape[0] // n_ylo
    for peer in range(n_ylo * n_cuts):
        row, column = peer // n_cuts * own_rows, peer % n_cuts * quarter
        out_ref[peer] = total[row : row + own_rows, column : column + quarter].astype(BF16)


def expert_rows(row_block, own, other, norm_gain, router, adapter_in, expert, counts):
    n_ylo, n_cuts, topk = counts
    width = norm_gain.shape[0]
    rows = row_block.shape[0]
    whole = pl.BlockSpec(memory_space=pltpu.VMEM)
    weights = own[:3] + other[:3]
    return pl.pallas_call(
        functools.partial(expert_kernel, n_ylo, n_cuts, topk),
        out_shape=jax.ShapeDtypeStruct((n_ylo * n_cuts, rows // n_ylo, width // n_cuts), BF16),
        in_specs=[pl.BlockSpec(memory_space=pltpu.SMEM)]
        + [whole] * 6
        + [pl.BlockSpec(memory_space=pl.ANY)] * len(weights),
        out_specs=whole,
        scratch_shapes=[
            pltpu.VMEM((len(weights),) + weights[0].shape, BF16),
            pltpu.SemaphoreType.DMA((len(weights),)),
        ],
        name="expert_rows",
    )(
        expert.reshape(1).astype(jnp.int32),
        pltpu.with_memory_space_constraint(row_block, pltpu.VMEM),
        norm_gain[None],
        router.T,
        adapter_in.T,
        own[3],
        other[3],
        *weights,
    )


def shards(
    queries,
    cache_keys,
    cache_values,
    new_keys,
    new_values,
    lengths,
    head_sinks,
    attn_proj,
    residual_in,
    norm_gain,
    router,
    expert_routes,
    expert_gate,
    expert_up,
    expert_down,
    adapter_in,
    adapter_gate,
    adapter_up,
):
    planes = lax.axis_size("z")
    n_cuts = lax.axis_size("cuts")
    n_side = lax.axis_size("side")
    n_ylo = lax.axis_size("ylo")
    side = lax.axis_index("side")
    plane = lax.axis_index("z")
    ylo = lax.axis_index("ylo")
    cut = lax.axis_index("cuts")
    rows, width = residual_in.shape
    topk = expert_routes.shape[1]
    heads_in, piece = attn_proj.shape
    strip = width // planes
    quarter = width // n_cuts
    swap = [(0, 1), (1, 0)]

    pieces = [attn_proj.T]
    for axes in ("core", "ylo", ("ylo", "core")):
        flip = swap if isinstance(axes, str) else [(i, 3 - i) for i in range(4)]
        pieces.append(lax.ppermute(attn_proj.T, axes, flip))
    core = lax.axis_index("core")
    pieces = [jnp.where(core == 0, pieces[i], pieces[i ^ 1]) for i in range(4)]
    pieces = [jnp.where(ylo == 0, pieces[i], pieces[i ^ 2]) for i in range(4)]
    plane_proj = jnp.concatenate(pieces, 0)
    adapters = jnp.concatenate([adapter_gate, adapter_up], 0)
    hidden_own = (expert_gate.T, expert_up.T, expert_down, adapters)
    hidden_other = tuple(lax.ppermute(part, "core", swap) for part in hidden_own)

    attn_out = attention_rows(
        queries, cache_keys, cache_values, new_keys, new_values, lengths, head_sinks
    )

    residual = residual_in.reshape(rows, planes, n_cuts, piece)
    residual = lax.dynamic_index_in_dim(residual, cut, 2, keepdims=False).transpose(1, 0, 2)
    payload = jnp.concatenate(
        [
            jnp.broadcast_to(attn_out[None], (planes, rows, heads_in)),
            residual,
            jnp.broadcast_to(expert_routes.astype(BF16)[None], (planes, rows, topk)),
            jnp.zeros((planes, rows, 128 - piece - topk), BF16),
        ],
        axis=2,
    )
    held = exchange(payload, "z")
    held = held.reshape(planes * rows, heads_in + 128)
    line = lax.broadcasted_iota(jnp.int32, (strip, 128), 1)
    column = lax.broadcasted_iota(jnp.int32, (strip, 128), 0)
    residual_part = jnp.where((column == cut * piece + line) & (line < piece), 1.0 / n_side, 0.0)
    weights = jnp.concatenate([plane_proj, residual_part.astype(BF16)], 1)
    partial = lax.dot_general(held, weights, (((1,), (1,)), ((), ())), preferred_element_type=F32)
    partial = partial.astype(BF16).reshape(1, n_cuts, rows * planes // n_cuts, strip)
    partial = jnp.broadcast_to(partial, (n_side,) + partial.shape[1:])
    partial = exchange(partial.reshape((n_side * n_cuts,) + partial.shape[2:]), ("side", "cuts"))
    middle = jnp.sum(partial.astype(F32), axis=0).astype(BF16)

    blocks = planes // n_cuts
    experts = side * planes + jnp.arange(planes)
    routes = held[:, heads_in + piece : heads_in + piece + topk].reshape(n_cuts, blocks, rows, topk)
    routes = lax.dynamic_index_in_dim(routes, cut, 0, keepdims=False)
    hot = slot_hot(routes.astype(jnp.int32), experts)
    source = jnp.concatenate([middle.reshape(blocks, rows, strip), routes], 2)
    outgoing = jnp.einsum("zktr,krd->zktd", hot, source, preferred_element_type=F32).astype(BF16)
    outgoing = outgoing.reshape(planes, blocks * CAP, strip + topk)
    arrived = exchange(outgoing, "z")
    row_part = arrived[:, :, :strip].transpose(1, 0, 2).reshape(blocks * CAP, width)
    lanes = -(-(width + topk) // 128) * 128
    spare = jnp.zeros((blocks * CAP, lanes - width - topk), BF16)
    row_part = jnp.concatenate([row_part, arrived[0, :, strip:], spare], 1)
    peers = n_ylo * n_cuts
    row_block = exchange(jnp.broadcast_to(row_part[None], (peers,) + row_part.shape), ("ylo", "cuts"))
    row_block = row_block.reshape(-1, lanes)

    expert = side * planes + plane
    value = expert_rows(
        row_block,
        hidden_own,
        hidden_other,
        norm_gain,
        router,
        adapter_in,
        expert,
        (n_ylo, n_cuts, topk),
    )

    own_rows = row_block.shape[0] // n_ylo
    value = exchange(value, ("ylo", "cuts"))
    total = jnp.sum(value.astype(F32), axis=0)
    mine = lax.dynamic_slice_in_dim(row_block, ylo * own_rows, own_rows)
    first = (mine[:, width].astype(jnp.int32) == expert).astype(F32)
    own_middle = lax.dynamic_slice_in_dim(mine, cut * quarter, quarter, 1).astype(F32)
    total = (total + own_middle * first[:, None]).astype(BF16)
    returned = exchange(total.reshape(planes, CAP, quarter), "z")
    own_hot = slot_hot(expert_routes[None], experts)[:, 0]
    out = jnp.einsum("etr,etd->rd", own_hot, returned, preferred_element_type=F32).astype(BF16)
    other = lax.ppermute(out, "side", swap)
    return (out.astype(F32) + other.astype(F32)).astype(BF16)


def solution(mesh):
    fine = Mesh(mesh.devices.reshape(2, 16, 2, 2, 4), ("side", "z", "ylo", "core", "cuts"))
    group = ("z", "ylo", "core")
    heads = ("side", "cuts")
    hidden = ("side", "z", "ylo", "core", "cuts")
    placed = (
        P(group, heads),
        P(group, heads, None, None),
        P(group, heads, None, None),
        P(group, heads),
        P(group, heads),
        P(group),
        P(heads),
        P(heads, group),
        P(group, None),
        P(),
        P(),
        P(group, None),
        P(None, hidden),
        P(None, hidden),
        P(hidden, None),
        P(),
        P(None, hidden),
        P(None, hidden),
    )

    return jax.shard_map(
        shards, mesh=fine, in_specs=placed, out_specs=P(group, "cuts"), check_vma=False
    )
```

```python
import functools
import math

import jax
import jax.numpy as jnp
from jax import lax
from jax.experimental import pallas as pl
from jax.experimental.pallas import tpu as pltpu
from jax.sharding import Mesh, PartitionSpec as P

CAP = 4
EPSILON = 1e-05
F32 = jnp.float32
BF16 = jnp.bfloat16


def attention_rows(queries, cache_keys, cache_values, new_keys, new_values, lengths, head_sinks):
    req_count = queries.shape[0]
    kv_count = cache_keys.shape[1]
    head_dim = cache_keys.shape[2]
    cache_len = cache_keys.shape[3]
    head_count = head_sinks.shape[0]
    group_size = head_count // kv_count
    query_rows = queries.reshape(req_count, kv_count, group_size, head_dim)
    fresh_key = new_keys.reshape(req_count, kv_count, head_dim)
    fresh_value = new_values.reshape(req_count, kv_count, head_dim)
    scaling = 1.0 / math.sqrt(head_dim)
    scores = (
        jnp.einsum("rkgd,rkdl->rkgl", query_rows, cache_keys, preferred_element_type=F32) * scaling
    )
    own_score = (
        jnp.einsum("rkgd,rkd->rkg", query_rows, fresh_key, preferred_element_type=F32) * scaling
    )
    validity = (
        lax.broadcasted_iota(jnp.int32, (req_count, 1, 1, cache_len), 3)
        < lengths[:, None, None, None]
    )
    scores = jnp.where(validity, scores, -1e30)
    sink_logit = head_sinks.reshape(1, kv_count, group_size)
    highest = jnp.maximum(jnp.maximum(jnp.max(scores, axis=3), own_score), sink_logit)
    exp_terms = jnp.where(validity, jnp.exp(scores - highest[..., None]), 0.0)
    own_term = jnp.exp(own_score - highest)
    denominator = jnp.sum(exp_terms, axis=3) + own_term + jnp.exp(sink_logit - highest)
    attn_probs = (exp_terms / denominator[..., None]).astype(BF16)
    own_prob = (own_term / denominator).astype(BF16)
    attn_mix = jnp.einsum("rkgl,rkdl->rkgd", attn_probs, cache_values, preferred_element_type=F32)
    attn_mix = attn_mix + own_prob.astype(F32)[..., None] * fresh_value.astype(F32)[:, :, None, :]
    return attn_mix.astype(BF16).reshape(req_count, head_count * head_dim)


def exchange(array, axes):
    return lax.all_to_all(array, axes, split_axis=0, concat_axis=0, tiled=True)


def slot_hot(routes, experts):
    rows = routes.shape[1]
    member = jnp.any(routes[None] == experts[:, None, None, None], axis=3)
    earlier = (
        lax.broadcasted_iota(jnp.int32, (rows, rows), 0)
        < lax.broadcasted_iota(jnp.int32, (rows, rows), 1)
    ).astype(BF16)
    before = jnp.einsum(
        "ebr,rq->ebq", member.astype(BF16), earlier, preferred_element_type=F32
    ).astype(jnp.int32)
    slots = lax.broadcasted_iota(jnp.int32, (1, 1, CAP, 1), 2)
    return (member[:, :, None, :] & (before[:, :, None, :] == slots)).astype(BF16)


def expert_kernel(n_ylo, n_cuts, topk, *refs):
    (expert_ref, rows_ref, gain_ref, router_ref, low_ref, *rest) = refs
    adapters, weights = rest[:2], rest[2:8]
    out_ref, held, sems = rest[8:]
    copies = [
        pltpu.make_async_copy(weights[i], held.at[i], sems.at[i]) for i in range(len(weights))
    ]
    for copy in copies:
        copy.start()
    width = gain_ref.shape[1]
    quarter = width // n_cuts
    nt = (((1,), (1,)), ((), ()))
    middle = rows_ref[:, :width].astype(F32)
    inverse = lax.rsqrt(jnp.mean(middle * middle, axis=1, keepdims=True) + EPSILON)
    normed = (middle * inverse * gain_ref[...]).astype(BF16)
    raw = jax.nn.sigmoid(lax.dot_general(normed, router_ref[...], nt, preferred_element_type=F32))
    names = lax.broadcasted_iota(jnp.int32, raw.shape, 1)
    named = names < 0
    for entry in range(topk):
        route = rows_ref[:, width + entry : width + entry + 1].astype(F32).astype(jnp.int32)
        named = named | (names == route)
    own = jnp.sum(jnp.where(names == expert_ref[0], raw, 0.0), axis=1, keepdims=True)
    row_weight = own / jnp.sum(jnp.where(named, raw, 0.0), axis=1, keepdims=True)
    low_code = lax.dot_general(normed, low_ref[...], nt, preferred_element_type=F32).astype(BF16)
    rank = low_ref.shape[0]
    total = None
    for half in range(2):
        copies[3 * half].wait()
        pre_gate = lax.dot_general(normed, held[3 * half], nt, preferred_element_type=F32)
        pre_gate = pre_gate + jnp.dot(
            low_code, adapters[half][:rank], preferred_element_type=F32
        )
        copies[3 * half + 1].wait()
        pre_up = lax.dot_general(normed, held[3 * half + 1], nt, preferred_element_type=F32)
        pre_up = pre_up + jnp.dot(low_code, adapters[half][rank:], preferred_element_type=F32)
        activated = (pre_up + 1.0) * pre_gate * jax.nn.sigmoid(1.702 * pre_gate)
        copies[3 * half + 2].wait()
        part = jnp.dot(activated.astype(BF16), held[3 * half + 2], preferred_element_type=F32)
        total = part if total is None else total + part
    total = total * row_weight
    own_rows = total.shape[0] // n_ylo
    for peer in range(n_ylo * n_cuts):
        row, column = peer // n_cuts * own_rows, peer % n_cuts * quarter
        out_ref[peer] = total[row : row + own_rows, column : column + quarter].astype(BF16)


def expert_rows(row_block, own, other, norm_gain, router, adapter_in, expert, counts):
    n_ylo, n_cuts, topk = counts
    width = norm_gain.shape[0]
    rows = row_block.shape[0]
    whole = pl.BlockSpec(memory_space=pltpu.VMEM)
    weights = own[:3] + other[:3]
    return pl.pallas_call(
        functools.partial(expert_kernel, n_ylo, n_cuts, topk),
        out_shape=jax.ShapeDtypeStruct((n_ylo * n_cuts, rows // n_ylo, width // n_cuts), BF16),
        in_specs=[pl.BlockSpec(memory_space=pltpu.SMEM)]
        + [whole] * 6
        + [pl.BlockSpec(memory_space=pl.ANY)] * len(weights),
        out_specs=whole,
        scratch_shapes=[
            pltpu.VMEM((len(weights),) + weights[0].shape, BF16),
            pltpu.SemaphoreType.DMA((len(weights),)),
        ],
        name="expert_rows",
    )(
        expert.reshape(1).astype(jnp.int32),
        pltpu.with_memory_space_constraint(row_block, pltpu.VMEM),
        norm_gain[None],
        router.T,
        adapter_in.T,
        own[3],
        other[3],
        *weights,
    )


def shards(
    queries,
    cache_keys,
    cache_values,
    new_keys,
    new_values,
    lengths,
    head_sinks,
    attn_proj,
    residual_in,
    norm_gain,
    router,
    expert_routes,
    expert_gate,
    expert_up,
    expert_down,
    adapter_in,
    adapter_gate,
    adapter_up,
):
    pairs = lax.axis_size("zp")
    planes = pairs * lax.axis_size("zq")
    n_cuts = lax.axis_size("cuts")
    n_side = lax.axis_size("side")
    n_ylo = lax.axis_size("ylo")
    side = lax.axis_index("side")
    plane = lax.axis_index(("zp", "zq"))
    odd = lax.axis_index("zq")
    ylo = lax.axis_index("ylo")
    core = lax.axis_index("core")
    cut = lax.axis_index("cuts")
    rows, width = residual_in.shape
    topk = expert_routes.shape[1]
    heads_in, _ = attn_proj.shape
    strip = width // pairs
    share = strip // n_cuts
    quarter = width // n_cuts
    swap = [(0, 1), (1, 0)]

    pair = [attn_proj.T, lax.ppermute(attn_proj.T, "zq", swap)]
    pair = jnp.stack([jnp.where(odd == i, pair[0], pair[1]) for i in range(2)])
    pieces = [pair]
    for axes in ("core", "ylo", ("ylo", "core")):
        flip = swap if isinstance(axes, str) else [(i, 3 - i) for i in range(4)]
        pieces.append(lax.ppermute(pair, axes, flip))
    pieces = [jnp.where(core == 0, pieces[i], pieces[i ^ 1]) for i in range(4)]
    pieces = [jnp.where(ylo == 0, pieces[i], pieces[i ^ 2]) for i in range(4)]
    pair_proj = jnp.stack(pieces, 1).reshape(strip, heads_in)
    adapters = jnp.concatenate([adapter_gate, adapter_up], 0)
    hidden_own = (expert_gate.T, expert_up.T, expert_down, adapters)
    hidden_other = tuple(lax.ppermute(part, "core", swap) for part in hidden_own)

    attn_out = attention_rows(
        queries, cache_keys, cache_values, new_keys, new_values, lengths, head_sinks
    )

    residual = residual_in.reshape(rows, pairs, n_cuts, share)
    residual = lax.dynamic_index_in_dim(residual, cut, 2, keepdims=False).transpose(1, 0, 2)
    payload = jnp.concatenate(
        [
            jnp.broadcast_to(attn_out[None], (pairs, rows, heads_in)),
            residual,
            jnp.broadcast_to(expert_routes.astype(BF16)[None], (pairs, rows, topk)),
            jnp.zeros((pairs, rows, 128 - share - topk), BF16),
        ],
        axis=2,
    )
    held = exchange(payload, "zp")
    held = held.reshape(pairs * rows, heads_in + 128)
    line = lax.broadcasted_iota(jnp.int32, (strip, 128), 1)
    column = lax.broadcasted_iota(jnp.int32, (strip, 128), 0)
    residual_part = jnp.where((column == cut * share + line) & (line < share), 1.0 / n_side, 0.0)
    weights = jnp.concatenate([pair_proj, residual_part.astype(BF16)], 1)
    partial = lax.dot_general(held, weights, (((1,), (1,)), ((), ())), preferred_element_type=F32)
    partial = partial.astype(BF16).reshape(1, n_cuts, rows * pairs // n_cuts, strip)
    partial = jnp.broadcast_to(partial, (n_side,) + partial.shape[1:])
    partial = exchange(partial.reshape((n_side * n_cuts,) + partial.shape[2:]), ("side", "cuts"))
    middle = jnp.sum(partial.astype(F32), axis=0).astype(BF16)

    blocks = pairs // n_cuts
    experts = side * planes + jnp.arange(planes)
    routes = held[:, heads_in + share : heads_in + share + topk].reshape(n_cuts, blocks, rows, topk)
    routes = lax.dynamic_index_in_dim(routes, cut, 0, keepdims=False)
    hot = slot_hot(routes.astype(jnp.int32), experts)
    source = jnp.concatenate([middle.reshape(blocks, rows, strip), routes], 2)
    outgoing = jnp.einsum("zktr,krd->zktd", hot, source, preferred_element_type=F32).astype(BF16)
    arrived = exchange(outgoing.reshape(planes, blocks * CAP, strip + topk), ("zp", "zq"))
    arrived = arrived.reshape(pairs, planes // pairs, blocks, CAP, strip + topk)
    row_part = arrived[..., :strip].transpose(2, 1, 3, 0, 4).reshape(-1, width)
    slot_routes = arrived[0, ..., strip:].transpose(1, 0, 2, 3).reshape(-1, topk)
    lanes = -(-(width + topk) // 128) * 128
    spare = jnp.zeros((row_part.shape[0], lanes - width - topk), BF16)
    row_part = jnp.concatenate([row_part, slot_routes, spare], 1)
    peers = n_ylo * n_cuts
    row_block = exchange(jnp.broadcast_to(row_part[None], (peers,) + row_part.shape), ("ylo", "cuts"))
    row_block = row_block.reshape(-1, lanes)

    expert = side * planes + plane
    value = expert_rows(
        row_block,
        hidden_own,
        hidden_other,
        norm_gain,
        router,
        adapter_in,
        expert,
        (n_ylo, n_cuts, topk),
    )

    own_rows = row_block.shape[0] // n_ylo
    value = exchange(value, ("ylo", "cuts"))
    total = jnp.sum(value.astype(F32), axis=0)
    mine = lax.dynamic_slice_in_dim(row_block, ylo * own_rows, own_rows)
    first = (mine[:, width].astype(jnp.int32) == expert).astype(F32)
    own_middle = lax.dynamic_slice_in_dim(mine, cut * quarter, quarter, 1).astype(F32)
    total = (total + own_middle * first[:, None]).astype(BF16)
    returned = exchange(total.reshape(planes, CAP, quarter), ("zp", "zq"))
    own_hot = slot_hot(expert_routes[None], experts)[:, 0]
    out = jnp.einsum("etr,etd->rd", own_hot, returned, preferred_element_type=F32).astype(BF16)
    other = lax.ppermute(out, "side", swap)
    return (out.astype(F32) + other.astype(F32)).astype(BF16)


def solution(mesh):
    names = ("side", "zp", "zq", "ylo", "core", "cuts")
    fine = Mesh(mesh.devices.reshape(2, 8, 2, 2, 2, 4), names)
    group = ("zp", "zq", "ylo", "core")
    heads = ("side", "cuts")
    hidden = names
    placed = (
        P(group, heads),
        P(group, heads, None, None),
        P(group, heads, None, None),
        P(group, heads),
        P(group, heads),
        P(group),
        P(heads),
        P(heads, group),
        P(group, None),
        P(),
        P(),
        P(group, None),
        P(None, hidden),
        P(None, hidden),
        P(hidden, None),
        P(),
        P(None, hidden),
        P(None, hidden),
    )

    return jax.shard_map(
        shards, mesh=fine, in_specs=placed, out_specs=P(group, "cuts"), check_vma=False
    )
```

```python
import functools
import math

import jax
import jax.numpy as jnp
from jax import lax
from jax.experimental import pallas as pl
from jax.experimental.pallas import tpu as pltpu
from jax.sharding import Mesh, PartitionSpec as P

CAP = 4
EPSILON = 1e-05
F32 = jnp.float32
BF16 = jnp.bfloat16


def attention_rows(queries, cache_keys, cache_values, new_keys, new_values, lengths, head_sinks):
    req_count = queries.shape[0]
    kv_count = cache_keys.shape[1]
    head_dim = cache_keys.shape[2]
    cache_len = cache_keys.shape[3]
    head_count = head_sinks.shape[0]
    group_size = head_count // kv_count
    query_rows = queries.reshape(req_count, kv_count, group_size, head_dim)
    fresh_key = new_keys.reshape(req_count, kv_count, head_dim)
    fresh_value = new_values.reshape(req_count, kv_count, head_dim)
    scaling = 1.0 / math.sqrt(head_dim)
    scores = (
        jnp.einsum("rkgd,rkdl->rkgl", query_rows, cache_keys, preferred_element_type=F32) * scaling
    )
    validity = (
        lax.broadcasted_iota(jnp.int32, (req_count, 1, 1, cache_len), 3)
        < lengths[:, None, None, None]
    )
    scores = jnp.where(validity, scores, -1e30)
    sink_logit = head_sinks.reshape(1, kv_count, group_size)
    peak = jnp.max(scores, axis=3)
    peak, fresh_key = lax.optimization_barrier((peak, fresh_key))
    own_score = (
        jnp.einsum("rkgd,rkd->rkg", query_rows, fresh_key, preferred_element_type=F32) * scaling
    )
    highest = jnp.maximum(jnp.maximum(peak, own_score), sink_logit)
    exp_terms = jnp.where(validity, jnp.exp(scores - highest[..., None]), 0.0)
    own_term = jnp.exp(own_score - highest)
    denominator = jnp.sum(exp_terms, axis=3) + own_term + jnp.exp(sink_logit - highest)
    attn_probs = (exp_terms / denominator[..., None]).astype(BF16)
    own_prob = (own_term / denominator).astype(BF16)
    attn_mix = jnp.einsum("rkgl,rkdl->rkgd", attn_probs, cache_values, preferred_element_type=F32)
    attn_mix = attn_mix + own_prob.astype(F32)[..., None] * fresh_value.astype(F32)[:, :, None, :]
    return attn_mix.astype(BF16).reshape(req_count, head_count * head_dim)


def exchange(array, axes):
    return lax.all_to_all(array, axes, split_axis=0, concat_axis=0, tiled=True)


def slot_hot(routes, experts):
    rows = routes.shape[1]
    member = jnp.any(routes[None] == experts[:, None, None, None], axis=3)
    earlier = (
        lax.broadcasted_iota(jnp.int32, (rows, rows), 0)
        < lax.broadcasted_iota(jnp.int32, (rows, rows), 1)
    ).astype(BF16)
    before = jnp.einsum(
        "ebr,rq->ebq", member.astype(BF16), earlier, preferred_element_type=F32
    ).astype(jnp.int32)
    slots = lax.broadcasted_iota(jnp.int32, (1, 1, CAP, 1), 2)
    return (member[:, :, None, :] & (before[:, :, None, :] == slots)).astype(BF16)


def expert_kernel(n_ylo, n_cuts, topk, *refs):
    (expert_ref, rows_ref, gain_ref, router_ref, low_ref, *rest) = refs
    adapters, weights = rest[:2], rest[2:8]
    out_ref, held, sems = rest[8:]
    units = held.shape[1]
    step = -(-units // (16 * 2)) * 16
    copies = []
    for i in range(len(weights)):
        for j, first in enumerate(range(0, units, step)):
            span = pl.ds(first, min(step, units - first))
            sem = sems.at[i, j]
            copies.append(pltpu.make_async_copy(weights[i].at[span], held.at[i, span], sem))
    parts = len(copies) // len(weights)
    for copy in copies[:6]:
        copy.start()

    def fetched(i):
        for j in range(i * parts, (i + 1) * parts):
            copies[j].wait()
            if j + 6 < len(copies):
                copies[j + 6].start()
        return held[i]

    width = gain_ref.shape[1]
    quarter = width // n_cuts
    nt = (((1,), (1,)), ((), ()))
    middle = rows_ref[:, :width].astype(F32)
    inverse = lax.rsqrt(jnp.mean(middle * middle, axis=1, keepdims=True) + EPSILON)
    normed = (middle * inverse * gain_ref[...]).astype(BF16)
    raw = jax.nn.sigmoid(lax.dot_general(normed, router_ref[...], nt, preferred_element_type=F32))
    names = lax.broadcasted_iota(jnp.int32, raw.shape, 1)
    named = names < 0
    for entry in range(topk):
        route = rows_ref[:, width + entry : width + entry + 1].astype(F32).astype(jnp.int32)
        named = named | (names == route)
    own = jnp.sum(jnp.where(names == expert_ref[0], raw, 0.0), axis=1, keepdims=True)
    row_weight = own / jnp.sum(jnp.where(named, raw, 0.0), axis=1, keepdims=True)
    low_code = lax.dot_general(normed, low_ref[...], nt, preferred_element_type=F32).astype(BF16)
    rank = low_ref.shape[0]
    total = None
    for half in range(2):
        pre_gate = lax.dot_general(normed, fetched(3 * half), nt, preferred_element_type=F32)
        pre_gate = pre_gate + jnp.dot(
            low_code, adapters[half][:rank], preferred_element_type=F32
        )
        pre_up = lax.dot_general(normed, fetched(3 * half + 1), nt, preferred_element_type=F32)
        pre_up = pre_up + jnp.dot(low_code, adapters[half][rank:], preferred_element_type=F32)
        activated = (pre_up + 1.0) * pre_gate * jax.nn.sigmoid(1.702 * pre_gate)
        part = jnp.dot(activated.astype(BF16), fetched(3 * half + 2), preferred_element_type=F32)
        total = part if total is None else total + part
    total = total * row_weight
    own_rows = total.shape[0] // n_ylo
    for peer in range(n_ylo * n_cuts):
        row, column = peer // n_cuts * own_rows, peer % n_cuts * quarter
        out_ref[peer] = total[row : row + own_rows, column : column + quarter].astype(BF16)


def expert_rows(row_block, own, other, norm_gain, router, adapter_in, expert, counts):
    n_ylo, n_cuts, topk = counts
    width = norm_gain.shape[0]
    rows = row_block.shape[0]
    whole = pl.BlockSpec(memory_space=pltpu.VMEM)
    weights = own[:3] + other[:3]
    return pl.pallas_call(
        functools.partial(expert_kernel, n_ylo, n_cuts, topk),
        out_shape=jax.ShapeDtypeStruct((n_ylo * n_cuts, rows // n_ylo, width // n_cuts), BF16),
        in_specs=[pl.BlockSpec(memory_space=pltpu.SMEM)]
        + [whole] * 6
        + [pl.BlockSpec(memory_space=pl.ANY)] * len(weights),
        out_specs=whole,
        scratch_shapes=[
            pltpu.VMEM((len(weights),) + weights[0].shape, BF16),
            pltpu.SemaphoreType.DMA((len(weights), 2)),
        ],
        name="expert_rows",
    )(
        expert.reshape(1).astype(jnp.int32),
        *(
            pltpu.with_memory_space_constraint(array, pltpu.VMEM)
            for array in (row_block, norm_gain[None], router.T, adapter_in.T, own[3], other[3])
        ),
        *weights,
    )


def shards(
    queries,
    cache_keys,
    cache_values,
    new_keys,
    new_values,
    lengths,
    head_sinks,
    attn_proj,
    residual_in,
    norm_gain,
    router,
    expert_routes,
    expert_gate,
    expert_up,
    expert_down,
    adapter_in,
    adapter_gate,
    adapter_up,
):
    pairs = lax.axis_size("zp")
    planes = pairs * lax.axis_size("zq")
    n_cuts = lax.axis_size("cuts")
    n_side = lax.axis_size("side")
    n_ylo = lax.axis_size("ylo")
    side = lax.axis_index("side")
    plane = lax.axis_index(("zp", "zq"))
    odd = lax.axis_index("zq")
    ylo = lax.axis_index("ylo")
    core = lax.axis_index("core")
    cut = lax.axis_index("cuts")
    rows, width = residual_in.shape
    topk = expert_routes.shape[1]
    heads_in, _ = attn_proj.shape
    strip = width // pairs
    share = strip // n_cuts
    quarter = width // n_cuts
    swap = [(0, 1), (1, 0)]

    attn_out = attention_rows(
        queries, cache_keys, cache_values, new_keys, new_values, lengths, head_sinks
    )

    own_proj, attn_out = lax.optimization_barrier((attn_proj.T, attn_out))
    pair = [own_proj, lax.ppermute(own_proj, "zq", swap)]
    pair = jnp.stack([jnp.where(odd == i, pair[0], pair[1]) for i in range(2)])
    pieces = [pair]
    for axes in ("core", "ylo", ("ylo", "core")):
        flip = swap if isinstance(axes, str) else [(i, 3 - i) for i in range(4)]
        pieces.append(lax.ppermute(pair, axes, flip))
    pieces = [jnp.where(core == 0, pieces[i], pieces[i ^ 1]) for i in range(4)]
    pieces = [jnp.where(ylo == 0, pieces[i], pieces[i ^ 2]) for i in range(4)]
    pair_proj = jnp.stack(pieces, 1).reshape(strip, heads_in)
    adapters = jnp.concatenate([adapter_gate, adapter_up], 0)
    hidden_own = (expert_gate.T, expert_up.T, expert_down, adapters)
    hidden_other = []
    for part in hidden_own:
        hidden_other.append(lax.ppermute(part, "core", swap))
    hidden_other = tuple(hidden_other)

    residual = residual_in.reshape(rows, pairs, n_cuts, share)
    residual = lax.dynamic_index_in_dim(residual, cut, 2, keepdims=False).transpose(1, 0, 2)
    payload = jnp.concatenate(
        [
            jnp.broadcast_to(attn_out[None], (pairs, rows, heads_in)),
            residual,
            jnp.broadcast_to(expert_routes.astype(BF16)[None], (pairs, rows, topk)),
            jnp.zeros((pairs, rows, 128 - share - topk), BF16),
        ],
        axis=2,
    )
    held = exchange(payload, "zp")
    held = held.reshape(pairs * rows, heads_in + 128)
    line = lax.broadcasted_iota(jnp.int32, (strip, 128), 1)
    column = lax.broadcasted_iota(jnp.int32, (strip, 128), 0)
    residual_part = jnp.where((column == cut * share + line) & (line < share), 1.0 / n_side, 0.0)
    weights = jnp.concatenate([pair_proj, residual_part.astype(BF16)], 1)
    partial = lax.dot_general(held, weights, (((1,), (1,)), ((), ())), preferred_element_type=F32)
    partial = partial.astype(BF16).reshape(1, n_cuts, rows * pairs // n_cuts, strip)
    partial = jnp.broadcast_to(partial, (n_side,) + partial.shape[1:])
    partial = partial.reshape((n_side * n_cuts,) + partial.shape[2:])
    partial = exchange(partial, ("side", "cuts"))
    middle = jnp.sum(partial.astype(F32), axis=0).astype(BF16)

    blocks = pairs // n_cuts
    experts = side * planes + jnp.arange(planes)
    routes = held[:, heads_in + share : heads_in + share + topk].reshape(n_cuts, blocks, rows, topk)
    routes = lax.dynamic_index_in_dim(routes, cut, 0, keepdims=False)
    hot = slot_hot(routes.astype(jnp.int32), experts)
    source = jnp.concatenate([middle.reshape(blocks, rows, strip), routes], 2)
    outgoing = jnp.einsum("zktr,krd->zktd", hot, source, preferred_element_type=F32).astype(BF16)
    outgoing = outgoing.reshape(planes, blocks * CAP, strip + topk)
    arrived = exchange(outgoing, ("zp", "zq"))
    arrived = arrived.reshape(pairs, planes // pairs, blocks, CAP, strip + topk)
    row_part = arrived[..., :strip].transpose(2, 1, 3, 0, 4).reshape(-1, width)
    slot_routes = arrived[0, ..., strip:].transpose(1, 0, 2, 3).reshape(-1, topk)
    lanes = -(-(width + topk) // 128) * 128
    spare = jnp.zeros((row_part.shape[0], lanes - width - topk), BF16)
    row_part = jnp.concatenate([row_part, slot_routes, spare], 1)
    peers = n_ylo * n_cuts
    row_part = jnp.broadcast_to(row_part[None], (peers,) + row_part.shape)
    row_block = exchange(row_part, ("ylo", "cuts"))
    row_block = row_block.reshape(-1, lanes)

    expert = side * planes + plane
    value = expert_rows(
        row_block,
        hidden_own,
        hidden_other,
        norm_gain,
        router,
        adapter_in,
        expert,
        (n_ylo, n_cuts, topk),
    )

    own_rows = row_block.shape[0] // n_ylo
    value = exchange(value, ("ylo", "cuts"))
    total = jnp.sum(value.astype(F32), axis=0)
    mine = lax.dynamic_slice_in_dim(row_block, ylo * own_rows, own_rows)
    first = (mine[:, width].astype(jnp.int32) == expert).astype(F32)
    own_middle = lax.dynamic_slice_in_dim(mine, cut * quarter, quarter, 1).astype(F32)
    total = (total + own_middle * first[:, None]).astype(BF16)
    returned = exchange(total.reshape(planes, CAP, quarter), ("zp", "zq"))
    own_hot = slot_hot(expert_routes[None], experts)[:, 0]
    out = jnp.einsum("etr,etd->rd", own_hot, returned, preferred_element_type=F32).astype(BF16)
    other = lax.ppermute(out, "side", swap)
    return (out.astype(F32) + other.astype(F32)).astype(BF16)


def solution(mesh):
    names = ("side", "zp", "zq", "ylo", "core", "cuts")
    fine = Mesh(mesh.devices.reshape(2, 8, 2, 2, 2, 4), names)
    group = ("zp", "zq", "ylo", "core")
    heads = ("side", "cuts")
    hidden = names
    placed = (
        P(group, heads),
        P(group, heads, None, None),
        P(group, heads, None, None),
        P(group, heads),
        P(group, heads),
        P(group),
        P(heads),
        P(heads, group),
        P(group, None),
        P(),
        P(),
        P(group, None),
        P(None, hidden),
        P(None, hidden),
        P(hidden, None),
        P(),
        P(None, hidden),
        P(None, hidden),
    )

    return jax.shard_map(
        shards, mesh=fine, in_specs=placed, out_specs=P(group, "cuts"), check_vma=False
    )
```
